32 devices in a mesh: grp: 2 (over y), row: 16 (over z, x, core).
Axes of the slice: x: 2, y: 2, z: 4, core: 2. Of those that a mesh axis runs over, the one named last changes fastest.
Arguments:
- features: float32 [128, 32, 512], P(('grp', 'row')), parts along dimension 0, may hold values from -6 to 6
- cotangent: float32 [128, 32, 512], P(('grp', 'row')), parts along dimension 0, may hold values from -8 to 8
- kernel: float32 [7, 7, 512], replicated, may hold values from -0.875 to 0.875
- norm_gain: float32 [512], replicated, may hold values from 0.1 to 1.9
- norm_bias: float32 [512], replicated, may hold values from -3 to 3
- in_weight: float32 [512, 2048], P('row'), may hold values from -0.25 to 0.25
- in_bias: float32 [2048], replicated, may hold values from -3 to 3
- out_weight: float32 [512, 2048], P('row'), may hold values from -0.125 to 0.125
- layer_scale: float32 [512], replicated, may hold values from 0.3 to 1.5
Outputs:
- output: float32 [128, 32, 512], P(('grp', 'row')), parts along dimension 0
- input_grad: float32 [128, 32, 512], P(('grp', 'row')), parts along dimension 0
- in_weight_grad: float32 [1024, 2048], P(('grp', 'row')), parts along dimension 0
- out_weight_grad: float32 [1024, 2048], P(('grp', 'row')), parts along dimension 0
- kernel_grad: float32 [14, 7, 512], P('grp'), parts along dimension 0
- gain_grad: float32 [1024], P('grp'), parts along dimension 0
- bias_grad: float32 [1024], P('grp'), parts along dimension 0
- in_bias_grad: float32 [4096], P('grp'), parts along dimension 0
- scale_grad: float32 [1024], P('grp'), parts along dimension 0
The draws below stay inside these ranges and needn't reach their ends.
There are 2 independent parts, one for each index of `grp`. The reference program is written for one: setup_inputs(seed, part) draws one part's arguments, and reference() takes and returns one part's arrays. A program takes and returns all parts, laid end to end along the dimension named above; an argument that names none is the same for every part. Nothing has to cross between parts.
All inputs are finite; a program needn't handle non-finite values.
Results may differ from the reference program's by a relative error of at most 0.0071.
Values may be sent and summed in bfloat16 or wider, within the bound.
A program may use at most 64 MiB of HBM per device.

```python
import math
import jax
import jax.numpy as jnp
from jax import lax

C = 512
FF = 2048
COLS = 32
TAPS = 7
ROWS = 64


def strengthened(entries, stream_key, source, target, shards_of, factor):
    def block_of(dim):
        return (jnp.arange(entries.shape[dim]) // (entries.shape[dim] // shards_of)).reshape((-1,) + (1,) * (entries.ndim - 1 - dim))

    first = jax.random.permutation(stream_key, shards_of)[block_of(target)]
    other_side = (block_of(target) + shards_of // 2) % shards_of
    return jnp.where((block_of(source) == first) | (block_of(source) == other_side), factor * entries, entries)


def steps_of(rng, dims, split, smallest, high):
    loudness, own = 1.0, jax.random.fold_in(rng, 6)
    for dim, parts in split:
        draws = jnp.exp(jax.random.uniform(jax.random.fold_in(own, dim), (parts,), jnp.float32, smallest / len(split), high / len(split)))
        loudness = loudness * jnp.repeat(draws, dims[dim] // parts).reshape([-1 if axis == dim else 1 for axis in range(len(dims))])
    return loudness


def scatter_about(rng, extent, spread, limit, cuts=(), dtype=jnp.bfloat16):
    gain = steps_of(rng, extent, cuts, -0.22, 0.18) if cuts else 1.0
    result = jax.random.normal(rng, extent, jnp.float32) * spread * gain
    return jnp.minimum(jnp.maximum(result, -limit), limit).astype(dtype)


def noise_with(rng, shape, scale, bound, pieces, heavy, held_as=jnp.bfloat16):
    result = scale * jax.random.normal(rng, shape, jnp.float32)
    if pieces:
        result = result * steps_of(rng, shape, pieces, -0.22, 0.18)
    return jnp.clip(strengthened(result, jax.random.fold_in(rng, 3), *heavy), -bound, bound).astype(held_as)


def setup_inputs(seed: int = 0, part: int = 0) -> dict:
    key_of = jax.random.split(jax.random.key(seed), 10)
    part_splits = jax.random.split(jax.random.fold_in(key_of[9], part), 10)
    return {
        "features": scatter_about(part_splits[0], (ROWS, COLS, C), 1.0, 6.0, ((0, 16),), jnp.float32),
        "cotangent": noise_with(part_splits[1], (ROWS, COLS, C), 1.0, 8.0, ((0, 16),), (0, 2, 16, 2.0), jnp.float32),
        "kernel": scatter_about(key_of[2], (TAPS, TAPS, C), (TAPS * TAPS) ** -0.5, 0.875, (), jnp.float32),
        "norm_gain": jnp.clip(1.0 + 0.18 * jax.random.normal(key_of[3], (C,), jnp.float32), 0.1, 1.9),
        "norm_bias": scatter_about(key_of[4], (C,), 0.5, 3.0, (), jnp.float32),
        "in_weight": scatter_about(key_of[5], (C, FF), C ** -0.5, 0.25, ((0, 16),), jnp.float32),
        "in_bias": scatter_about(key_of[6], (FF,), 0.5, 3.0, (), jnp.float32),
        "out_weight": scatter_about(key_of[7], (C, FF), FF ** -0.5, 0.125, ((0, 16),), jnp.float32),
        "layer_scale": jnp.clip(jnp.exp(jax.random.uniform(key_of[8], (C,), jnp.float32, math.log(0.3), math.log(1.5))), 0.3, 1.5),
    }


def conv_taps(padded, kernel, row_count, col_count):
    running = jnp.zeros((row_count, col_count, padded.shape[2]), jnp.float32)
    for tap_row in range(7):
        for tap_col in range(7):
            running = running + padded[tap_row:tap_row + row_count, tap_col:tap_col + col_count] * kernel[tap_row, tap_col]
    return running

def reference(features, cotangent, kernel, norm_gain, norm_bias, in_weight, in_bias, out_weight, layer_scale):
    row_count, col_count, channels = features.shape
    hidden_count = in_weight.shape[1]
    norm_scale = 1.0 / math.sqrt(row_count * col_count)
    padded = jnp.pad(features, ((3, 3), (3, 3), (0, 0)))
    convolved = conv_taps(padded, kernel, row_count, col_count).reshape(-1, channels)
    pixel_count = row_count * col_count
    block_size = math.gcd(pixel_count, 8192)
    block_total = pixel_count // block_size
    in_narrow = in_weight.astype(jnp.bfloat16)
    out_narrow = out_weight.astype(jnp.bfloat16)
    conv_blocks = convolved.reshape(block_total, block_size, channels)
    input_blocks = features.reshape(block_total, block_size, channels)
    cotan_blocks = cotangent.reshape(block_total, block_size, channels)

    def step_block(running, inputs):
        conv_part, input_part, cotan_part = inputs
        average = lax.optimization_barrier(jnp.mean(conv_part, axis=1, keepdims=True))
        centred = conv_part - average
        inv_std = lax.rsqrt(lax.optimization_barrier(jnp.mean(centred * centred, axis=1, keepdims=True)) + 1e-06)
        normed = centred * inv_std
        normed_out = (normed * norm_gain + norm_bias).astype(jnp.bfloat16)
        preact = jnp.dot(normed_out, in_narrow, preferred_element_type=jnp.float32) + in_bias
        cdf_value = 0.5 * (1.0 + jax.scipy.special.erf(preact * 0.7071067811865476))
        activated = (preact * cdf_value).astype(jnp.bfloat16)
        mixed = lax.dot_general(activated, out_narrow, (((1,), (1,)), ((), ())), preferred_element_type=jnp.float32)
        output_part = input_part + layer_scale * mixed
        scale_term = lax.optimization_barrier(jnp.sum(cotan_part * mixed, axis=0))
        branch_grad = (layer_scale * cotan_part).astype(jnp.bfloat16)
        out_term = lax.dot_general(branch_grad, activated, (((0,), (0,)), ((), ())), preferred_element_type=jnp.float32)
        act_grad = jnp.dot(branch_grad, out_narrow, preferred_element_type=jnp.float32)
        gelu_slope = cdf_value + preact * jnp.exp(-0.5 * preact * preact) * 0.3989422804014327
        hidden_grad = act_grad * gelu_slope
        in_bias_term = lax.optimization_barrier(jnp.sum(hidden_grad, axis=0))
        hidden_narrow = hidden_grad.astype(jnp.bfloat16)
        in_term = lax.dot_general(normed_out, hidden_narrow, (((0,), (0,)), ((), ())), preferred_element_type=jnp.float32)
        out_grad = lax.dot_general(hidden_narrow, in_narrow, (((1,), (1,)), ((), ())), preferred_element_type=jnp.float32)
        gain_term = lax.optimization_barrier(jnp.sum(out_grad * normed, axis=0))
        bias_term = lax.optimization_barrier(jnp.sum(out_grad, axis=0))
        normed_grad = out_grad * norm_gain
        conv_grad = inv_std * (normed_grad - lax.optimization_barrier(jnp.mean(normed_grad, axis=1, keepdims=True)) - normed * lax.optimization_barrier(jnp.mean(normed_grad * normed, axis=1, keepdims=True)))
        updated = (running[0] + in_term, running[1] + out_term, running[2] + gain_term, running[3] + bias_term, running[4] + in_bias_term, running[5] + scale_term)
        return (updated, (output_part, conv_grad))
    initial = (jnp.zeros((channels, hidden_count), jnp.float32), jnp.zeros((channels, hidden_count), jnp.float32), jnp.zeros((channels,), jnp.float32), jnp.zeros((channels,), jnp.float32), jnp.zeros((hidden_count,), jnp.float32), jnp.zeros((channels,), jnp.float32))
    sums, stacked = lax.scan(step_block, initial, (conv_blocks, input_blocks, cotan_blocks))
    output = stacked[0].reshape(row_count, col_count, channels)
    conv_grad = stacked[1].reshape(row_count, col_count, channels)
    grad_padded = jnp.pad(conv_grad, ((3, 3), (3, 3), (0, 0)))
    input_grad = cotangent
    kernel_rows = []
    for tap_row in range(7):
        tap_list = []
        for tap_col in range(7):
            input_grad = input_grad + kernel[tap_row, tap_col] * grad_padded[6 - tap_row:6 - tap_row + row_count, 6 - tap_col:6 - tap_col + col_count]
            tap_list.append(lax.optimization_barrier(jnp.sum(padded[tap_row:tap_row + row_count, tap_col:tap_col + col_count] * conv_grad, axis=(0, 1))))
        kernel_rows.append(jnp.stack(tap_list))
    kernel_grad = norm_scale * jnp.stack(kernel_rows)
    return (output, input_grad, norm_scale * sums[0], norm_scale * sums[1], kernel_grad, norm_scale * sums[2], norm_scale * sums[3], norm_scale * sums[4], norm_scale * sums[5])
```

```python
import functools
import math

import jax
import jax.numpy as jnp
from jax import lax
from jax.experimental import pallas as pl
from jax.experimental.pallas import tpu as pltpu
from jax.sharding import PartitionSpec as P


def extended(block, sides, width):
    for axis, dim in sides:
        count = lax.axis_size(axis)
        forward = [(i, i + 1) for i in range(count - 1)]
        backward = [(target, source) for source, target in forward]
        low = lax.ppermute(
            lax.slice_in_dim(block, block.shape[dim] - width, None, axis=dim), axis, forward
        )
        high = lax.ppermute(lax.slice_in_dim(block, 0, width, axis=dim), axis, backward)
        block = jnp.concatenate([low, block, high], axis=dim)
    return block


def conv_taps(padded, kernel, row_count, col_count):
    running = jnp.zeros((row_count, col_count, padded.shape[2]), jnp.float32)
    for tap_row in range(7):
        for tap_col in range(7):
            running = (
                running
                + padded[tap_row : tap_row + row_count, tap_col : tap_col + col_count]
                * kernel[tap_row, tap_col]
            )
    return running


def contract_last(left, right):
    return lax.dot_general(
        left, right, (((1,), (1,)), ((), ())), preferred_element_type=jnp.float32
    )


def contract_first(left, right):
    return lax.dot_general(
        left, right, (((0,), (0,)), ((), ())), preferred_element_type=jnp.float32
    )


def per_device(
    features, cotangent, kernel, norm_gain, norm_bias, in_weight, in_bias, out_weight, layer_scale
):
    row_count, col_count, channels = features.shape
    hidden_count = in_weight.shape[1]
    norm_scale = 1.0 / math.sqrt(row_count * col_count * lax.axis_size("row"))
    rimmed = extended(features, (("row", 0),), 3)
    padded = jnp.pad(rimmed, ((0, 0), (3, 3), (0, 0)))
    convolved = conv_taps(padded, kernel, row_count, col_count).reshape(-1, channels)
    average = jnp.mean(convolved, axis=1, keepdims=True)
    centred = convolved - average
    inv_std = lax.rsqrt(jnp.mean(centred * centred, axis=1, keepdims=True) + 1e-06)
    normed = centred * inv_std
    normed_out = (normed * norm_gain + norm_bias).astype(jnp.bfloat16)
    in_narrow = in_weight.astype(jnp.bfloat16)
    out_narrow = out_weight.astype(jnp.bfloat16)

    def fold_rows(left, piece):
        return jnp.dot(left, piece, preferred_element_type=jnp.float32)

    def map_rows(left, piece):
        return contract_last(left, piece)

    preact = fold_rows(normed_out, lax.all_gather(in_narrow, "row", axis=0, tiled=True)) + in_bias
    cdf_value = 0.5 * (1.0 + jax.scipy.special.erf(preact * 0.7071067811865476))
    activated = (preact * cdf_value).astype(jnp.bfloat16)
    mixed = map_rows(activated, lax.all_gather(out_narrow, "row", axis=0, tiled=True))
    flat_input = features.reshape(-1, channels)
    flat_cotan = cotangent.reshape(-1, channels)
    output = (flat_input + layer_scale * mixed).reshape(row_count, col_count, channels)
    scale_term = jnp.sum(flat_cotan * mixed, axis=0)
    branch_grad = (layer_scale * flat_cotan).astype(jnp.bfloat16)
    act_grad = fold_rows(branch_grad, lax.all_gather(out_narrow, "row", axis=0, tiled=True))
    gelu_slope = cdf_value + preact * jnp.exp(-0.5 * preact * preact) * 0.3989422804014327
    hidden_grad = act_grad * gelu_slope
    in_bias_term = jnp.sum(hidden_grad, axis=0)
    hidden_narrow = hidden_grad.astype(jnp.bfloat16)
    out_grad = map_rows(hidden_narrow, lax.all_gather(in_narrow, "row", axis=0, tiled=True))
    gain_term = jnp.sum(out_grad * normed, axis=0)
    bias_term = jnp.sum(out_grad, axis=0)
    normed_grad = out_grad * norm_gain
    conv_grad = inv_std * (
        normed_grad
        - jnp.mean(normed_grad, axis=1, keepdims=True)
        - normed * jnp.mean(normed_grad * normed, axis=1, keepdims=True)
    )
    grad_pairs = lax.psum_scatter(
        jnp.concatenate(
            [
                norm_scale * contract_first(normed_out, hidden_narrow),
                norm_scale * contract_first(branch_grad, activated),
            ],
            axis=1,
        ),
        "row",
        scatter_dimension=0,
        tiled=True,
    )
    in_weight_grad = grad_pairs[:, :hidden_count]
    out_weight_grad = grad_pairs[:, hidden_count:]
    conv_grid = conv_grad.reshape(row_count, col_count, channels)
    grad_rimmed = extended(conv_grid, (("row", 0),), 3)
    grad_padded = jnp.pad(grad_rimmed, ((0, 0), (3, 3), (0, 0)))
    input_grad = cotangent
    kernel_rows = []
    for tap_row in range(7):
        tap_list = []
        for tap_col in range(7):
            input_grad = (
                input_grad
                + kernel[tap_row, tap_col]
                * grad_padded[
                    6 - tap_row : 6 - tap_row + row_count, 6 - tap_col : 6 - tap_col + col_count
                ]
            )
            tap_list.append(
                jnp.sum(
                    padded[tap_row : tap_row + row_count, tap_col : tap_col + col_count]
                    * conv_grid,
                    axis=(0, 1),
                )
            )
        kernel_rows.append(jnp.stack(tap_list))
    kernel_term = norm_scale * jnp.stack(kernel_rows)
    small_sums = lax.psum(
        (
            kernel_term,
            norm_scale * gain_term,
            norm_scale * bias_term,
            norm_scale * in_bias_term,
            norm_scale * scale_term,
        ),
        "row",
    )
    return (
        output,
        input_grad,
        in_weight_grad,
        out_weight_grad,
        small_sums[0],
        small_sums[1],
        small_sums[2],
        small_sums[3],
        small_sums[4],
    )


F32, BF16 = jnp.float32, jnp.bfloat16
MESH = pl.DeviceIdType.MESH
CORES, XS = 2, 2
LANES = 128
EDGE = 8


def fits(count):
    planes = count // (CORES * XS)
    return count % (CORES * XS) == 0 and planes == 4


def per_device_fused(
    features, cotangent, kernel, norm_gain, norm_bias, in_weight, in_bias, out_weight, layer_scale
):
    count = lax.axis_size("row")
    planes = count // (CORES * XS)
    rows, cols, channels = features.shape
    own, hidden = in_weight.shape
    pixels = rows * cols
    taps = kernel.shape[0]
    rim = taps // 2
    wide = cols + 2 * EDGE
    chunk = channels
    pieces = hidden // chunk
    tap_total = taps * taps
    bias_rows = hidden // channels
    small_rows = tap_total + 3 + bias_rows
    norm_scale = 1.0 / math.sqrt(pixels * count)

    def body(
        feat, cot, kern, gain, beta, w_in, b_in, w_out, scale,
        out, in_grad, gw_in, gw_out, small_out,
        weights, grads, from_core, x_send, from_x, z_send, from_up, from_down, line_sum,
        padded, grad_padded, grad_edge, conv, normed_s, inv_s, no_s, no_t, bg_s, bg_t, mixed_s, og_s,
        small, from_small,
        s_ag, r_ag, s_core, r_core, s_x, r_x, s_z, r_up, r_down,
        s_halo, r_halo, s_ghalo, r_ghalo, s_small, r_small,
    ):
        me = lax.axis_index("row")
        core = lax.rem(me, CORES)
        xpos = lax.rem(me // CORES, XS)
        z = me // (CORES * XS)
        sibling = me + 1 - 2 * core
        across = me + CORES - 2 * CORES * xpos
        step_z = CORES * XS

        def at(zz, xx, cc):
            return (zz * XS + xx) * CORES + cc

        def copy(src, dst, send, recv, target):
            return pltpu.make_async_remote_copy(
                src_ref=src, dst_ref=dst, send_sem=send, recv_sem=recv,
                device_id={"row": target}, device_id_type=MESH,
            )

        has_up, has_down = z < planes - 1, z > 0
        has_next, has_prev = me < count - 1, me > 0
        far_z = z + 2 - 4 * lax.rem(z // 2, 2)
        near_z = z + 1 - 2 * lax.rem(z, 2)
        far, near = at(far_z, xpos, core), at(near_z, xpos, core)

        weights[0, me] = w_in[...].astype(BF16)
        weights[1, me] = w_out[...].astype(BF16)

        barrier = pltpu.get_barrier_semaphore()

        def greet(target):
            pl.semaphore_signal(barrier, inc=1, device_id={"row": target}, device_id_type=MESH)

        outer = lax.rem(me + count + 2 * core - 1, count)
        peers = [sibling, across, outer]
        peers += [at(lax.rem(z + d, planes), xpos, core) for d in range(1, planes)]
        for target in peers:
            greet(target)
        pl.semaphore_wait(barrier, len(peers))

        halo_next = copy(
            feat.at[rows - rim :], padded.at[0:rim, EDGE : EDGE + cols],
            s_halo.at[0], r_halo.at[0], lax.rem(me + 1, count),
        )
        halo_prev = copy(
            feat.at[0:rim], padded.at[rows + rim :, EDGE : EDGE + cols],
            s_halo.at[1], r_halo.at[1], lax.rem(me + count - 1, count),
        )

        @pl.when(has_next)
        def _():
            halo_next.start()

        @pl.when(has_prev)
        def _():
            halo_prev.start()

        def block(r):
            return weights.at[:, r]

        def ag(r, way, target):
            return copy(block(r), block(r), s_ag.at[way, r], r_ag.at[r], target)

        def arrived(r):
            ag(r, 0, sibling).wait_recv()

        started = []

        def send_if(here, r, way, target):
            if here is True:
                ag(r, way, target).start()
            else:
                @pl.when(here)
                def _():
                    ag(r, way, target).start()
            started.append((here, r, way, target))

        send_if(has_up, me, 0, me + step_z)
        send_if(has_down, me, 1, me - step_z)
        send_if(True, me, 2, across)
        send_if(True, me, 3, sibling)

        def gather_line(d):
            for sign in (1, -1):
                zz = z - sign * d
                here = (zz >= 0) & (zz < planes)
                r = at(zz, xpos, core)
                onward = has_up if sign > 0 else has_down

                @pl.when(here)
                def _():
                    arrived(r)

                send_if(here & onward, r, 0 if sign > 0 else 1, me + sign * step_z)
                send_if(here, r, 2, across)
                send_if(here, r, 3, sibling)

        def gather_across(d):
            for sign in (1, -1) if d else (1,):
                zz = z - sign * d
                here = (zz >= 0) & (zz < planes)
                r = at(zz, 1 - xpos, core)

                @pl.when(here)
                def _():
                    arrived(r)

                send_if(here, r, 3, sibling)

        blank = jnp.zeros((rows + 2 * rim, EDGE, channels), F32)
        for pad in (padded, grad_padded):
            pad[:, 0:EDGE, :] = blank
            pad[:, EDGE + cols :, :] = blank
        no_rows = jnp.zeros((rim, cols, channels), F32)
        padded[rim : rim + rows, EDGE : EDGE + cols, :] = feat[...]
        for here, first in ((has_prev, 0), (has_next, rows + rim)):
            @pl.when(jnp.logical_not(here))
            def _():
                padded[first : first + rim, EDGE : EDGE + cols, :] = no_rows
                grad_padded[first : first + rim, EDGE : EDGE + cols, :] = no_rows
        scaled = scale[...] * cot[...].reshape(pixels, channels)
        bg_s[...] = scaled.astype(BF16)
        bg_t[...] = scaled.T.astype(BF16)

        @pl.when(has_prev)
        def _():
            halo_next.wait_recv()

        @pl.when(has_next)
        def _():
            halo_prev.wait_recv()

        def lanes_of(i):
            return pl.ds(pl.multiple_of(i * LANES, LANES), LANES)

        def tap_sums(source, lanes, flip, starts):
            sums = list(starts)
            for j in range(taps):
                shift = EDGE - rim + j
                lines = [source[q, shift : shift + cols, lanes] for q in range(rows + 2 * rim)]
                for i in range(taps):
                    t = (taps - 1 - i) * taps + taps - 1 - j if flip else i * taps + j
                    weight = kern[t : t + 1, lanes]
                    for q in range(rows):
                        sums[q] = sums[q] + lines[q + i] * weight
            return sums

        def conv_step(i, carry):
            lanes = lanes_of(i)
            sums = tap_sums(padded, lanes, False, [jnp.zeros((cols, LANES), F32)] * rows)
            for q in range(rows):
                conv[q * cols : (q + 1) * cols, lanes] = sums[q]
            return carry

        lax.fori_loop(0, channels // LANES, conv_step, 0)
        gather_line(1)
        value = conv[...]
        centred = value - jnp.mean(value, axis=1, keepdims=True)
        inv_std = lax.rsqrt(jnp.mean(centred * centred, axis=1, keepdims=True) + 1e-06)
        normed = centred * inv_std
        normed_s[...] = normed
        inv_s[...] = jnp.broadcast_to(inv_std, inv_s.shape)
        rescaled = normed * gain[...] + beta[...]
        no_s[...] = rescaled.astype(BF16)
        no_t[...] = rescaled.T.astype(BF16)
        mixed_s[...] = jnp.zeros_like(mixed_s)
        og_s[...] = jnp.zeros_like(og_s)
        gather_across(0)
        for d in range(2, planes):
            gather_line(d)
            gather_across(d - 1)
        gather_across(planes - 1)
        for xx in (xpos, 1 - xpos):
            for zz in range(planes):
                arrived(at(zz, xx, 1 - core))

        def last_last(a, b):
            return lax.dot_general(a, b, (((1,), (1,)), ((), ())), preferred_element_type=F32)

        def mlp_step(p, carry):
            span = pl.ds(pl.multiple_of(p * chunk, chunk), chunk)
            win = weights[0, :, :, span].reshape(channels, chunk)
            wout = weights[1, :, :, span].reshape(channels, chunk)
            preact = jnp.dot(no_s[...], win, preferred_element_type=F32) + b_in[:, span]
            cdf = 0.5 * (1.0 + lax.erf(preact * 0.7071067811865476))
            activated = (preact * cdf).astype(BF16)
            act_grad = jnp.dot(bg_s[...], wout, preferred_element_type=F32)
            slope = cdf + preact * jnp.exp(-0.5 * preact * preact) * 0.3989422804014327
            hidden_grad = act_grad * slope
            small[pl.ds(tap_total + 3 + p, 1), :] = norm_scale * jnp.sum(
                hidden_grad, axis=0, keepdims=True
            )
            narrow = hidden_grad.astype(BF16)
            grads[:, 0, :, span] = (
                (norm_scale * jnp.dot(no_t[...], narrow, preferred_element_type=F32))
                .astype(BF16).reshape(count, own, chunk)
            )
            grads[:, 1, :, span] = (
                (norm_scale * jnp.dot(bg_t[...], activated, preferred_element_type=F32))
                .astype(BF16).reshape(count, own, chunk)
            )
            mixed_s[...] += last_last(activated, wout)
            og_s[...] += last_last(narrow, win)
            return carry

        lax.fori_loop(0, pieces, mlp_step, 0)

        order = []
        for d in range(planes - 1, 0, -1):
            for sign in (1, -1):
                zz = z + sign * d
                order.append((zz, (zz >= 0) & (zz < planes), sign))

        def each(run, xx):
            for zz, here, sign in order:
                @pl.when(here)
                def _():
                    run(zz, xx, sign)
            run(z, xx, 0)

        def core_copy(zz, xx):
            slot = zz * XS + xx
            return copy(
                grads.at[at(zz, xx, 1 - core)], from_core.at[slot],
                s_core.at[slot], r_core.at[slot], sibling,
            )

        def x_copy(zz):
            return copy(x_send.at[zz], from_x.at[zz], s_x.at[zz], r_x.at[zz], across)

        def up_copy(zz):
            return copy(
                z_send.at[zz], from_up.at[zz], s_z.at[zz], r_up.at[zz],
                at(lax.rem(z + 1, planes), xpos, core),
            )

        def down_copy(zz):
            return copy(
                z_send.at[zz], from_down.at[zz], s_z.at[zz], r_down.at[zz],
                at(lax.rem(z + planes - 1, planes), xpos, core),
            )

        each(lambda zz, xx, sign: core_copy(zz, xx).start(), 1 - xpos)
        each(lambda zz, xx, sign: core_copy(zz, xx).start(), xpos)

        flat_cot = cot[...].reshape(pixels, channels)
        mixed = mixed_s[...]
        out[...] = feat[...] + (scale[...] * mixed).reshape(rows, cols, channels)
        small[tap_total + 2 : tap_total + 3, :] = norm_scale * jnp.sum(
            flat_cot * mixed, axis=0, keepdims=True
        )
        out_grad = og_s[...]
        normed = normed_s[...]
        small[tap_total : tap_total + 1, :] = norm_scale * jnp.sum(
            out_grad * normed, axis=0, keepdims=True
        )
        small[tap_total + 1 : tap_total + 2, :] = norm_scale * jnp.sum(
            out_grad, axis=0, keepdims=True
        )
        normed_grad = out_grad * gain[...]
        conv_grad = inv_s[:, 0:1] * (
            normed_grad
            - jnp.mean(normed_grad, axis=1, keepdims=True)
            - normed * jnp.mean(normed_grad * normed, axis=1, keepdims=True)
        )
        grid = conv_grad.reshape(rows, cols, channels)
        grad_padded[rim : rim + rows, EDGE : EDGE + cols, :] = grid
        grad_edge[...] = grid
        ghalo_next = copy(
            grad_edge.at[rows - rim :], grad_padded.at[0:rim, EDGE : EDGE + cols],
            s_ghalo.at[0], r_ghalo.at[0], lax.rem(me + 1, count),
        )
        ghalo_prev = copy(
            grad_edge.at[0:rim], grad_padded.at[rows + rim :, EDGE : EDGE + cols],
            s_ghalo.at[1], r_ghalo.at[1], lax.rem(me + count - 1, count),
        )

        @pl.when(has_next)
        def _():
            ghalo_next.start()

        @pl.when(has_prev)
        def _():
            ghalo_prev.start()

        def add_for_x(zz, xx, sign):
            core_copy(zz, xx).wait_recv()
            x_send[zz] = (
                grads[at(zz, xx, core)].astype(F32) + from_core[zz * XS + xx].astype(F32)
            ).astype(BF16)
            x_copy(zz).start()

        each(add_for_x, 1 - xpos)

        def kernel_step(i, carry):
            lanes = lanes_of(i)
            lines_grad = [grad_edge[q, :, lanes] for q in range(rows)]
            for j in range(taps):
                shift = EDGE - rim + j
                lines = [padded[q, shift : shift + cols, lanes] for q in range(rows + 2 * rim)]
                for k in range(taps):
                    total = lines[k] * lines_grad[0]
                    for q in range(1, rows):
                        total = total + lines[k + q] * lines_grad[q]
                    t = k * taps + j
                    small[t : t + 1, lanes] = norm_scale * jnp.sum(total, axis=0, keepdims=True)
            return carry

        lax.fori_loop(0, channels // LANES, kernel_step, 0)

        hops = (sibling, across, near, far)

        def small_copy(h):
            return copy(
                small.at[h * small_pad : (h + 1) * small_pad], from_small.at[h],
                s_small.at[h], r_small.at[h], hops[h],
            )

        def small_add(h):
            small_copy(h).wait_recv()
            small[(h + 1) * small_pad : (h + 2) * small_pad] = (
                small[h * small_pad : (h + 1) * small_pad] + from_small[h]
            )
            if h + 1 < len(hops):
                small_copy(h + 1).start()

        small_copy(0).start()

        def add_for_line(zz, xx, sign):
            core_copy(zz, xx).wait_recv()
            line_sum[zz] = grads[at(zz, xx, core)].astype(F32) + from_core[zz * XS + xx].astype(F32)

        each(add_for_line, xpos)
        small_add(0)

        @pl.when(has_prev)
        def _():
            ghalo_next.wait_recv()

        @pl.when(has_next)
        def _():
            ghalo_prev.wait_recv()

        def back_step(i, carry):
            lanes = lanes_of(i)
            sums = tap_sums(grad_padded, lanes, True, [cot[q, :, lanes] for q in range(rows)])
            for q in range(rows):
                in_grad[q, :, lanes] = sums[q]
            return carry

        lax.fori_loop(0, channels // LANES, back_step, 0)
        small_add(1)

        def pass_on(zz, sign):
            x_copy(zz).wait_recv()
            line_sum[zz] = line_sum[zz] + from_x[zz].astype(F32)
            if sign > 0:
                @pl.when(has_down)
                def _():
                    up_copy(zz).wait_recv()
                    line_sum[zz] = line_sum[zz] + from_up[zz].astype(F32)
                z_send[zz] = line_sum[zz].astype(BF16)
                up_copy(zz).start()
            else:
                @pl.when(has_up)
                def _():
                    down_copy(zz).wait_recv()
                    line_sum[zz] = line_sum[zz] + from_down[zz].astype(F32)
                z_send[zz] = line_sum[zz].astype(BF16)
                down_copy(zz).start()

        for number, (zz, here, sign) in enumerate(order):
            @pl.when(here)
            def _():
                pass_on(zz, sign)
            if number == 1:
                small_add(2)
        small_add(3)
        small_out[...] = small[4 * small_pad : 5 * small_pad]
        x_copy(z).wait_recv()
        line_sum[z] = line_sum[z] + from_x[z].astype(F32)

        @pl.when(has_down)
        def _():
            up_copy(z).wait_recv()
            line_sum[z] = line_sum[z] + from_up[z].astype(F32)

        @pl.when(has_up)
        def _():
            down_copy(z).wait_recv()
            line_sum[z] = line_sum[z] + from_down[z].astype(F32)

        gw_in[...] = line_sum[z, 0]
        gw_out[...] = line_sum[z, 1]

        @pl.when(has_next)
        def _():
            halo_next.wait_send()
            ghalo_next.wait_send()

        @pl.when(has_prev)
        def _():
            halo_prev.wait_send()
            ghalo_prev.wait_send()

        for here, r, way, target in started:
            if here is True:
                ag(r, way, target).wait_send()
            else:
                @pl.when(here)
                def _():
                    ag(r, way, target).wait_send()
        for zz in range(planes):
            for xx in range(XS):
                core_copy(zz, xx).wait_send()
            x_copy(zz).wait_send()
        for zz, here, sign in order:
            @pl.when(here)
            def _():
                up_copy(zz).wait_send()
        for h in range(len(hops)):
            small_copy(h).wait_send()

    small_pad = -(-small_rows // 8) * 8
    vmem = pl.BlockSpec(memory_space=pltpu.VMEM)
    dma = pltpu.SemaphoreType.DMA
    whole = (rows + 2 * rim, wide, channels)
    pair = (2, own, hidden)
    results = pl.pallas_call(
        body,
        out_shape=(
            jax.ShapeDtypeStruct(features.shape, F32),
            jax.ShapeDtypeStruct(features.shape, F32),
            jax.ShapeDtypeStruct((own, hidden), F32),
            jax.ShapeDtypeStruct((own, hidden), F32),
            jax.ShapeDtypeStruct((small_pad, channels), F32),
        ),
        in_specs=[vmem] * 9,
        out_specs=[vmem] * 5,
        scratch_shapes=[
            pltpu.VMEM((2, count, own, hidden), BF16),
            pltpu.VMEM((count,) + pair, BF16),
            pltpu.VMEM((planes * XS,) + pair, BF16),
            pltpu.VMEM((planes,) + pair, BF16),
            pltpu.VMEM((planes,) + pair, BF16),
            pltpu.VMEM((planes,) + pair, BF16),
            pltpu.VMEM((planes,) + pair, BF16),
            pltpu.VMEM((planes,) + pair, BF16),
            pltpu.VMEM((planes,) + pair, F32),
            pltpu.VMEM(whole, F32),
            pltpu.VMEM(whole, F32),
            pltpu.VMEM(features.shape, F32),
            pltpu.VMEM((pixels, channels), F32),
            pltpu.VMEM((pixels, channels), F32),
            pltpu.VMEM((pixels, LANES), F32),
            pltpu.VMEM((pixels, channels), BF16),
            pltpu.VMEM((channels, pixels), BF16),
            pltpu.VMEM((pixels, channels), BF16),
            pltpu.VMEM((channels, pixels), BF16),
            pltpu.VMEM((pixels, channels), F32),
            pltpu.VMEM((pixels, channels), F32),
            pltpu.VMEM((5 * small_pad, channels), F32),
            pltpu.VMEM((4, small_pad, channels), F32),
            dma((4, count)),
            dma((count,)),
            dma((planes * XS,)),
            dma((planes * XS,)),
            dma((planes,)),
            dma((planes,)),
            dma((planes,)),
            dma((planes,)),
            dma((planes,)),
            dma((2,)),
            dma((2,)),
            dma((2,)),
            dma((2,)),
            dma((4,)),
            dma((4,)),
        ],
        compiler_params=pltpu.CompilerParams(collective_id=0, has_side_effects=True),
        name="convnext_block",
    )(
        features,
        cotangent,
        kernel.reshape(tap_total, channels),
        norm_gain.reshape(1, channels),
        norm_bias.reshape(1, channels),
        in_weight,
        in_bias.reshape(1, hidden),
        out_weight,
        layer_scale.reshape(1, channels),
    )
    output, input_grad, in_weight_grad, out_weight_grad, sums = results
    return (
        output,
        input_grad,
        in_weight_grad,
        out_weight_grad,
        sums[:tap_total].reshape(taps, taps, channels),
        sums[tap_total],
        sums[tap_total + 1],
        sums[tap_total + 3 : small_rows].reshape(hidden),
        sums[tap_total + 2],
    )


def solution(mesh):
    return jax.shard_map(
        per_device_fused if fits(mesh.shape["row"]) else per_device,
        mesh=mesh,
        in_specs=(
            P(("grp", "row"), None, None),
            P(("grp", "row"), None, None),
            P(),
            P(),
            P(),
            P("row", None),
            P(),
            P("row", None),
            P(),
        ),
        out_specs=(
            P(("grp", "row"), None, None),
            P(("grp", "row"), None, None),
            P(("grp", "row"), None),
            P(("grp", "row"), None),
            P("grp", None, None),
            P("grp"),
            P("grp"),
            P("grp"),
            P("grp"),
        ),
        check_vma=False,
    )
```

```python
import functools
import math

import jax
import jax.numpy as jnp
from jax import lax
from jax.experimental import pallas as pl
from jax.experimental.pallas import tpu as pltpu
from jax.sharding import PartitionSpec as P


def extended(block, sides, width):
    for axis, dim in sides:
        count = lax.axis_size(axis)
        forward = [(i, i + 1) for i in range(count - 1)]
        backward = [(target, source) for source, target in forward]
        low = lax.ppermute(
            lax.slice_in_dim(block, block.shape[dim] - width, None, axis=dim), axis, forward
        )
        high = lax.ppermute(lax.slice_in_dim(block, 0, width, axis=dim), axis, backward)
        block = jnp.concatenate([low, block, high], axis=dim)
    return block


def conv_taps(padded, kernel, row_count, col_count):
    running = jnp.zeros((row_count, col_count, padded.shape[2]), jnp.float32)
    for tap_row in range(7):
        for tap_col in range(7):
            running = (
                running
                + padded[tap_row : tap_row + row_count, tap_col : tap_col + col_count]
                * kernel[tap_row, tap_col]
            )
    return running


def contract_last(left, right):
    return lax.dot_general(
        left, right, (((1,), (1,)), ((), ())), preferred_element_type=jnp.float32
    )


def contract_first(left, right):
    return lax.dot_general(
        left, right, (((0,), (0,)), ((), ())), preferred_element_type=jnp.float32
    )


def per_device(
    features, cotangent, kernel, norm_gain, norm_bias, in_weight, in_bias, out_weight, layer_scale
):
    row_count, col_count, channels = features.shape
    hidden_count = in_weight.shape[1]
    norm_scale = 1.0 / math.sqrt(row_count * col_count * lax.axis_size("row"))
    rimmed = extended(features, (("row", 0),), 3)
    padded = jnp.pad(rimmed, ((0, 0), (3, 3), (0, 0)))
    convolved = conv_taps(padded, kernel, row_count, col_count).reshape(-1, channels)
    average = jnp.mean(convolved, axis=1, keepdims=True)
    centred = convolved - average
    inv_std = lax.rsqrt(jnp.mean(centred * centred, axis=1, keepdims=True) + 1e-06)
    normed = centred * inv_std
    normed_out = (normed * norm_gain + norm_bias).astype(jnp.bfloat16)
    in_narrow = in_weight.astype(jnp.bfloat16)
    out_narrow = out_weight.astype(jnp.bfloat16)

    def fold_rows(left, piece):
        return jnp.dot(left, piece, preferred_element_type=jnp.float32)

    def map_rows(left, piece):
        return contract_last(left, piece)

    preact = fold_rows(normed_out, lax.all_gather(in_narrow, "row", axis=0, tiled=True)) + in_bias
    cdf_value = 0.5 * (1.0 + jax.scipy.special.erf(preact * 0.7071067811865476))
    activated = (preact * cdf_value).astype(jnp.bfloat16)
    mixed = map_rows(activated, lax.all_gather(out_narrow, "row", axis=0, tiled=True))
    flat_input = features.reshape(-1, channels)
    flat_cotan = cotangent.reshape(-1, channels)
    output = (flat_input + layer_scale * mixed).reshape(row_count, col_count, channels)
    scale_term = jnp.sum(flat_cotan * mixed, axis=0)
    branch_grad = (layer_scale * flat_cotan).astype(jnp.bfloat16)
    act_grad = fold_rows(branch_grad, lax.all_gather(out_narrow, "row", axis=0, tiled=True))
    gelu_slope = cdf_value + preact * jnp.exp(-0.5 * preact * preact) * 0.3989422804014327
    hidden_grad = act_grad * gelu_slope
    in_bias_term = jnp.sum(hidden_grad, axis=0)
    hidden_narrow = hidden_grad.astype(jnp.bfloat16)
    out_grad = map_rows(hidden_narrow, lax.all_gather(in_narrow, "row", axis=0, tiled=True))
    gain_term = jnp.sum(out_grad * normed, axis=0)
    bias_term = jnp.sum(out_grad, axis=0)
    normed_grad = out_grad * norm_gain
    conv_grad = inv_std * (
        normed_grad
        - jnp.mean(normed_grad, axis=1, keepdims=True)
        - normed * jnp.mean(normed_grad * normed, axis=1, keepdims=True)
    )
    grad_pairs = lax.psum_scatter(
        jnp.concatenate(
            [
                norm_scale * contract_first(normed_out, hidden_narrow),
                norm_scale * contract_first(branch_grad, activated),
            ],
            axis=1,
        ),
        "row",
        scatter_dimension=0,
        tiled=True,
    )
    in_weight_grad = grad_pairs[:, :hidden_count]
    out_weight_grad = grad_pairs[:, hidden_count:]
    conv_grid = conv_grad.reshape(row_count, col_count, channels)
    grad_rimmed = extended(conv_grid, (("row", 0),), 3)
    grad_padded = jnp.pad(grad_rimmed, ((0, 0), (3, 3), (0, 0)))
    input_grad = cotangent
    kernel_rows = []
    for tap_row in range(7):
        tap_list = []
        for tap_col in range(7):
            input_grad = (
                input_grad
                + kernel[tap_row, tap_col]
                * grad_padded[
                    6 - tap_row : 6 - tap_row + row_count, 6 - tap_col : 6 - tap_col + col_count
                ]
            )
            tap_list.append(
                jnp.sum(
                    padded[tap_row : tap_row + row_count, tap_col : tap_col + col_count]
                    * conv_grid,
                    axis=(0, 1),
                )
            )
        kernel_rows.append(jnp.stack(tap_list))
    kernel_term = norm_scale * jnp.stack(kernel_rows)
    small_sums = lax.psum(
        (
            kernel_term,
            norm_scale * gain_term,
            norm_scale * bias_term,
            norm_scale * in_bias_term,
            norm_scale * scale_term,
        ),
        "row",
    )
    return (
        output,
        input_grad,
        in_weight_grad,
        out_weight_grad,
        small_sums[0],
        small_sums[1],
        small_sums[2],
        small_sums[3],
        small_sums[4],
    )


F32, BF16 = jnp.float32, jnp.bfloat16
MESH = pl.DeviceIdType.MESH
CORES, XS = 2, 2
LANES = 128
EDGE = 8


def fits(count):
    planes = count // (CORES * XS)
    return count % (CORES * XS) == 0 and planes == 4


def per_device_fused(
    features, cotangent, kernel, norm_gain, norm_bias, in_weight, in_bias, out_weight, layer_scale
):
    count = lax.axis_size("row")
    planes = count // (CORES * XS)
    rows, cols, channels = features.shape
    own, hidden = in_weight.shape
    pixels = rows * cols
    taps = kernel.shape[0]
    rim = taps // 2
    wide = cols + 2 * EDGE
    chunk = channels
    pieces = hidden // chunk
    tap_total = taps * taps
    bias_rows = hidden // channels
    small_rows = tap_total + 3 + bias_rows
    norm_scale = 1.0 / math.sqrt(pixels * count)

    def body(
        feat, cot, kern, gain, beta, w_in, b_in, w_out, scale,
        out, in_grad, gw_in, gw_out, taps_out, small_out,
        weights, grads, from_core, x_send, from_x, z_send, from_up, from_down,
        padded, grad_padded, grad_edge, feat_edge, edge_in, conv, normed_s, inv_s, no_s, no_t, bg_s, bg_t, mixed_s, og_s,
        small, from_small,
        s_ag, r_ag, s_core, r_core, s_x, r_x, s_z, r_up, r_down,
        s_halo, r_halo, s_ghalo, r_ghalo, s_small, r_small,
    ):
        me = lax.axis_index("row")
        core = lax.rem(me, CORES)
        xpos = lax.rem(me // CORES, XS)
        z = me // (CORES * XS)
        sibling = me + 1 - 2 * core
        across = me + CORES - 2 * CORES * xpos
        step_z = CORES * XS

        def at(zz, xx, cc):
            return (zz * XS + xx) * CORES + cc

        def copy(src, dst, send, recv, target):
            return pltpu.make_async_remote_copy(
                src_ref=src, dst_ref=dst, send_sem=send, recv_sem=recv,
                device_id={"row": target}, device_id_type=MESH,
            )

        has_up, has_down = z < planes - 1, z > 0
        has_next, has_prev = me < count - 1, me > 0
        far_z = z + 2 - 4 * lax.rem(z // 2, 2)
        near_z = z + 1 - 2 * lax.rem(z, 2)
        far, near = at(far_z, xpos, core), at(near_z, xpos, core)

        feat_edge[...] = feat[...].astype(BF16)
        weights[0, me] = w_in[...].astype(BF16)
        weights[1, me] = w_out[...].astype(BF16)

        barrier = pltpu.get_barrier_semaphore()

        def greet(target):
            pl.semaphore_signal(barrier, inc=1, device_id={"row": target}, device_id_type=MESH)

        outer = lax.rem(me + count + 2 * core - 1, count)
        peers = [sibling, across, outer]
        peers += [at(lax.rem(z + d, planes), xpos, core) for d in range(1, planes)]
        for target in peers:
            greet(target)
        pl.semaphore_wait(barrier, len(peers))

        halo_next = copy(
            feat_edge.at[rows - rim :], edge_in.at[0],
            s_halo.at[0], r_halo.at[0], lax.rem(me + 1, count),
        )
        halo_prev = copy(
            feat_edge.at[0:rim], edge_in.at[1],
            s_halo.at[1], r_halo.at[1], lax.rem(me + count - 1, count),
        )

        @pl.when(has_next)
        def _():
            halo_next.start()

        @pl.when(has_prev)
        def _():
            halo_prev.start()

        def block(r):
            return weights.at[:, r]

        def ag(r, way, target):
            return copy(block(r), block(r), s_ag.at[way, r], r_ag.at[r], target)

        def arrived(r):
            ag(r, 0, sibling).wait_recv()

        started = []

        def send_if(here, r, way, target):
            if here is True:
                ag(r, way, target).start()
            else:
                @pl.when(here)
                def _():
                    ag(r, way, target).start()
            started.append((here, r, way, target))

        send_if(has_up, me, 0, me + step_z)
        send_if(has_down, me, 1, me - step_z)
        send_if(True, me, 2, across)
        send_if(True, me, 3, sibling)

        def gather_line(d):
            for sign in (1, -1):
                zz = z - sign * d
                here = (zz >= 0) & (zz < planes)
                r = at(zz, xpos, core)
                onward = has_up if sign > 0 else has_down

                @pl.when(here)
                def _():
                    arrived(r)

                send_if(here & onward, r, 0 if sign > 0 else 1, me + sign * step_z)
                send_if(here, r, 2, across)
                send_if(here, r, 3, sibling)

        def gather_across(d):
            for sign in (1, -1) if d else (1,):
                zz = z - sign * d
                here = (zz >= 0) & (zz < planes)
                r = at(zz, 1 - xpos, core)

                @pl.when(here)
                def _():
                    arrived(r)

                send_if(here, r, 3, sibling)

        blank = jnp.zeros((rows + 2 * rim, EDGE, channels), F32)
        for pad in (padded, grad_padded):
            pad[:, 0:EDGE, :] = blank
            pad[:, EDGE + cols :, :] = blank
        no_rows = jnp.zeros((rim, cols, channels), F32)
        padded[rim : rim + rows, EDGE : EDGE + cols, :] = feat[...]
        for here, first in ((has_prev, 0), (has_next, rows + rim)):
            @pl.when(jnp.logical_not(here))
            def _():
                padded[first : first + rim, EDGE : EDGE + cols, :] = no_rows
                grad_padded[first : first + rim, EDGE : EDGE + cols, :] = no_rows
        scaled = scale[...] * cot[...].reshape(pixels, channels)
        bg_s[...] = scaled.astype(BF16)
        bg_t[...] = scaled.T.astype(BF16)

        @pl.when(has_prev)
        def _():
            halo_next.wait_recv()
            padded[0:rim, EDGE : EDGE + cols, :] = edge_in[0].astype(F32)

        @pl.when(has_next)
        def _():
            halo_prev.wait_recv()
            padded[rows + rim :, EDGE : EDGE + cols, :] = edge_in[1].astype(F32)

        def lanes_of(i):
            return pl.ds(pl.multiple_of(i * LANES, LANES), LANES)

        def tap_sums(source, lanes, flip, starts):
            sums = list(starts)
            for j in range(taps):
                shift = EDGE - rim + j
                lines = [source[q, shift : shift + cols, lanes] for q in range(rows + 2 * rim)]
                for i in range(taps):
                    ki, kj = (taps - 1 - i, taps - 1 - j) if flip else (i, j)
                    weight = kern[ki, kj : kj + 1, lanes]
                    for q in range(rows):
                        sums[q] = sums[q] + lines[q + i] * weight
            return sums

        def conv_step(i, carry):
            lanes = lanes_of(i)
            sums = tap_sums(padded, lanes, False, [jnp.zeros((cols, LANES), F32)] * rows)
            for q in range(rows):
                conv[q * cols : (q + 1) * cols, lanes] = sums[q]
            return carry

        lax.fori_loop(0, channels // LANES, conv_step, 0)
        gather_line(1)
        value = conv[...]
        centred = value - jnp.mean(value, axis=1, keepdims=True)
        inv_std = lax.rsqrt(jnp.mean(centred * centred, axis=1, keepdims=True) + 1e-06)
        normed = centred * inv_std
        normed_s[...] = normed
        inv_s[...] = jnp.broadcast_to(inv_std, inv_s.shape)
        rescaled = normed * gain[...] + beta[...]
        no_s[...] = rescaled.astype(BF16)
        no_t[...] = rescaled.T.astype(BF16)
        mixed_s[...] = jnp.zeros_like(mixed_s)
        og_s[...] = jnp.zeros_like(og_s)
        gather_across(0)
        for d in range(2, planes):
            gather_line(d)
            gather_across(d - 1)
        gather_across(planes - 1)
        for xx in (xpos, 1 - xpos):
            for zz in range(planes):
                arrived(at(zz, xx, 1 - core))

        def last_last(a, b):
            return lax.dot_general(a, b, (((1,), (1,)), ((), ())), preferred_element_type=F32)

        def mlp_step(p, carry):
            span = pl.ds(pl.multiple_of(p * chunk, chunk), chunk)
            win = weights[0, :, :, span].reshape(channels, chunk)
            wout = weights[1, :, :, span].reshape(channels, chunk)
            preact = jnp.dot(no_s[...], win, preferred_element_type=F32) + b_in[:, span]
            cdf = 0.5 * (1.0 + lax.erf(preact * 0.7071067811865476))
            activated = (preact * cdf).astype(BF16)
            act_grad = jnp.dot(bg_s[...], wout, preferred_element_type=F32)
            slope = cdf + preact * jnp.exp(-0.5 * preact * preact) * 0.3989422804014327
            hidden_grad = act_grad * slope
            small[pl.ds(tap_total + 3 + p, 1), :] = norm_scale * jnp.sum(
                hidden_grad, axis=0, keepdims=True
            )
            narrow = hidden_grad.astype(BF16)
            grads[:, 0, :, span] = (
                (norm_scale * jnp.dot(no_t[...], narrow, preferred_element_type=F32))
                .astype(BF16).reshape(count, own, chunk)
            )
            grads[:, 1, :, span] = (
                (norm_scale * jnp.dot(bg_t[...], activated, preferred_element_type=F32))
                .astype(BF16).reshape(count, own, chunk)
            )
            mixed_s[...] += last_last(activated, wout)
            og_s[...] += last_last(narrow, win)
            return carry

        lax.fori_loop(0, pieces, mlp_step, 0)

        order = []
        for d in range(planes - 1, 0, -1):
            for sign in (1, -1):
                zz = z + sign * d
                order.append((zz, (zz >= 0) & (zz < planes), sign))

        def each(run, xx):
            for zz, here, sign in order:
                @pl.when(here)
                def _():
                    run(zz, xx, sign)
            run(z, xx, 0)

        def core_copy(zz, xx):
            slot = zz * XS + xx
            return copy(
                grads.at[at(zz, xx, 1 - core)], from_core.at[slot],
                s_core.at[slot], r_core.at[slot], sibling,
            )

        def x_copy(zz):
            return copy(x_send.at[zz], from_x.at[zz], s_x.at[zz], r_x.at[zz], across)

        def up_copy(zz):
            return copy(
                z_send.at[zz], from_up.at[zz], s_z.at[zz], r_up.at[zz],
                at(lax.rem(z + 1, planes), xpos, core),
            )

        def down_copy(zz):
            return copy(
                z_send.at[zz], from_down.at[zz], s_z.at[zz], r_down.at[zz],
                at(lax.rem(z + planes - 1, planes), xpos, core),
            )

        far_order = order[: 2 * (planes - 2)]
        near_order = order[2 * (planes - 2) :]

        def each_of(entries, run, xx):
            for zz, here, sign in entries:
                @pl.when(here)
                def _():
                    run(zz, xx, sign)

        each(lambda zz, xx, sign: core_copy(zz, xx).start(), 1 - xpos)
        each(lambda zz, xx, sign: core_copy(zz, xx).start(), xpos)

        def pair_sum(zz, xx):
            core_copy(zz, xx).wait_recv()
            return grads[at(zz, xx, core)].astype(F32) + from_core[zz * XS + xx].astype(F32)

        def add_for_x(zz, xx, sign):
            x_send[zz] = pair_sum(zz, xx).astype(BF16)
            x_copy(zz).start()

        each_of(far_order, add_for_x, 1 - xpos)

        flat_cot = cot[...].reshape(pixels, channels)
        small[tap_total + 2 : tap_total + 3, :] = norm_scale * jnp.sum(
            flat_cot * mixed_s[...], axis=0, keepdims=True
        )
        out_grad = og_s[...]
        normed = normed_s[...]
        small[tap_total : tap_total + 1, :] = norm_scale * jnp.sum(
            out_grad * normed, axis=0, keepdims=True
        )
        small[tap_total + 1 : tap_total + 2, :] = norm_scale * jnp.sum(
            out_grad, axis=0, keepdims=True
        )
        normed_grad = out_grad * gain[...]
        conv_grad = inv_s[:, 0:1] * (
            normed_grad
            - jnp.mean(normed_grad, axis=1, keepdims=True)
            - normed * jnp.mean(normed_grad * normed, axis=1, keepdims=True)
        )
        grid = conv_grad.reshape(rows, cols, channels)
        grad_padded[rim : rim + rows, EDGE : EDGE + cols, :] = grid
        grad_edge[...] = grid.astype(BF16)
        ghalo_next = copy(
            grad_edge.at[rows - rim :], edge_in.at[2],
            s_ghalo.at[0], r_ghalo.at[0], lax.rem(me + 1, count),
        )
        ghalo_prev = copy(
            grad_edge.at[0:rim], edge_in.at[3],
            s_ghalo.at[1], r_ghalo.at[1], lax.rem(me + count - 1, count),
        )

        @pl.when(has_next)
        def _():
            ghalo_next.start()

        @pl.when(has_prev)
        def _():
            ghalo_prev.start()

        def kernel_step(i, carry):
            lanes = lanes_of(i)
            lines_grad = [
                grad_padded[rim + q, EDGE : EDGE + cols, lanes] for q in range(rows)
            ]
            for j in range(taps):
                shift = EDGE - rim + j
                lines = [padded[q, shift : shift + cols, lanes] for q in range(rows + 2 * rim)]
                for k in range(taps):
                    total = lines[k] * lines_grad[0]
                    for q in range(1, rows):
                        total = total + lines[k + q] * lines_grad[q]
                    t = k * taps + j
                    small[t : t + 1, lanes] = norm_scale * jnp.sum(total, axis=0, keepdims=True)
            return carry

        lax.fori_loop(0, channels // LANES, kernel_step, 0)

        hops = (sibling, across, near, far)

        def small_copy(h):
            return copy(
                small.at[h * small_pad : (h + 1) * small_pad], from_small.at[h],
                s_small.at[h], r_small.at[h], hops[h],
            )

        def small_add(h):
            small_copy(h).wait_recv()
            small[(h + 1) * small_pad : (h + 2) * small_pad] = (
                small[h * small_pad : (h + 1) * small_pad] + from_small[h]
            )
            if h + 1 < len(hops):
                small_copy(h + 1).start()

        small_copy(0).start()
        out[...] = feat[...] + (scale[...] * mixed_s[...]).reshape(rows, cols, channels)
        small_add(0)
        each_of(near_order, add_for_x, 1 - xpos)
        add_for_x(z, 1 - xpos, 0)

        def pass_on(zz, xx, sign):
            fed, arriving, leaving = (
                (has_down, up_copy(zz), up_copy(zz)) if sign > 0
                else (has_up, down_copy(zz), down_copy(zz))
            )
            slots = from_up if sign > 0 else from_down
            x_copy(zz).wait_recv()
            total = pair_sum(zz, xx) + from_x[zz].astype(F32)

            @pl.when(fed)
            def _():
                arriving.wait_recv()
                z_send[zz] = (total + slots[zz].astype(F32)).astype(BF16)

            @pl.when(jnp.logical_not(fed))
            def _():
                z_send[zz] = total.astype(BF16)

            leaving.start()

        each_of(far_order, pass_on, xpos)

        @pl.when(has_prev)
        def _():
            ghalo_next.wait_recv()
            grad_padded[0:rim, EDGE : EDGE + cols, :] = edge_in[2].astype(F32)

        @pl.when(has_next)
        def _():
            ghalo_prev.wait_recv()
            grad_padded[rows + rim :, EDGE : EDGE + cols, :] = edge_in[3].astype(F32)

        def back_step(i, carry):
            lanes = lanes_of(i)
            sums = tap_sums(grad_padded, lanes, True, [cot[q, :, lanes] for q in range(rows)])
            for q in range(rows):
                in_grad[q, :, lanes] = sums[q]
            return carry

        lax.fori_loop(0, channels // LANES, back_step, 0)
        small_add(1)
        each_of(near_order, pass_on, xpos)
        small_add(2)
        x_copy(z).wait_recv()
        mine = pair_sum(z, xpos) + from_x[z].astype(F32)
        gw_in[...] = mine[0]
        gw_out[...] = mine[1]

        def join(slots):
            gw_in[...] += slots[z, 0].astype(F32)
            gw_out[...] += slots[z, 1].astype(F32)

        small_add(3)
        last = 4 * small_pad
        for i in range(taps):
            taps_out[i] = small[last + i * taps : last + (i + 1) * taps]
        small_out[0 : small_rows - tap_total] = small[last + tap_total : last + small_rows]

        @pl.when(has_down)
        def _():
            up_copy(z).wait_recv()
            join(from_up)

        @pl.when(has_up)
        def _():
            down_copy(z).wait_recv()
            join(from_down)

        @pl.when(has_next)
        def _():
            halo_next.wait_send()
            ghalo_next.wait_send()

        @pl.when(has_prev)
        def _():
            halo_prev.wait_send()
            ghalo_prev.wait_send()

        for here, r, way, target in started:
            if here is True:
                ag(r, way, target).wait_send()
            else:
                @pl.when(here)
                def _():
                    ag(r, way, target).wait_send()
        for zz in range(planes):
            for xx in range(XS):
                core_copy(zz, xx).wait_send()
            x_copy(zz).wait_send()
        for zz, here, sign in order:
            @pl.when(here)
            def _():
                up_copy(zz).wait_send()
        for h in range(len(hops)):
            small_copy(h).wait_send()

    small_pad = -(-small_rows // 8) * 8
    vmem = pl.BlockSpec(memory_space=pltpu.VMEM)
    dma = pltpu.SemaphoreType.DMA
    whole = (rows + 2 * rim, wide, channels)
    pair = (2, own, hidden)
    results = pl.pallas_call(
        body,
        out_shape=(
            jax.ShapeDtypeStruct(features.shape, F32),
            jax.ShapeDtypeStruct(features.shape, F32),
            jax.ShapeDtypeStruct((own, hidden), F32),
            jax.ShapeDtypeStruct((own, hidden), F32),
            jax.ShapeDtypeStruct(kernel.shape, F32),
            jax.ShapeDtypeStruct((small_rows - tap_total, channels), F32),
        ),
        in_specs=[vmem] * 9,
        out_specs=[vmem] * 6,
        scratch_shapes=[
            pltpu.VMEM((2, count, own, hidden), BF16),
            pltpu.VMEM((count,) + pair, BF16),
            pltpu.VMEM((planes * XS,) + pair, BF16),
            pltpu.VMEM((planes,) + pair, BF16),
            pltpu.VMEM((planes,) + pair, BF16),
            pltpu.VMEM((planes,) + pair, BF16),
            pltpu.VMEM((planes,) + pair, BF16),
            pltpu.VMEM((planes,) + pair, BF16),
            pltpu.VMEM(whole, F32),
            pltpu.VMEM(whole, F32),
            pltpu.VMEM(features.shape, BF16),
            pltpu.VMEM(features.shape, BF16),
            pltpu.VMEM((4, rim, cols, channels), BF16),
            pltpu.VMEM((pixels, channels), F32),
            pltpu.VMEM((pixels, channels), F32),
            pltpu.VMEM((pixels, LANES), F32),
            pltpu.VMEM((pixels, channels), BF16),
            pltpu.VMEM((channels, pixels), BF16),
            pltpu.VMEM((pixels, channels), BF16),
            pltpu.VMEM((channels, pixels), BF16),
            pltpu.VMEM((pixels, channels), F32),
            pltpu.VMEM((pixels, channels), F32),
            pltpu.VMEM((5 * small_pad, channels), F32),
            pltpu.VMEM((4, small_pad, channels), F32),
            dma((4, count)),
            dma((count,)),
            dma((planes * XS,)),
            dma((planes * XS,)),
            dma((planes,)),
            dma((planes,)),
            dma((planes,)),
            dma((planes,)),
            dma((planes,)),
            dma((2,)),
            dma((2,)),
            dma((2,)),
            dma((2,)),
            dma((4,)),
            dma((4,)),
        ],
        compiler_params=pltpu.CompilerParams(collective_id=0, has_side_effects=True),
        name="convnext_block",
    )(
        features,
        cotangent,
        kernel,
        norm_gain.reshape(1, channels),
        norm_bias.reshape(1, channels),
        in_weight,
        in_bias.reshape(1, hidden),
        out_weight,
        layer_scale.reshape(1, channels),
    )
    output, input_grad, in_weight_grad, out_weight_grad, kernel_grad, sums = results
    return (
        output,
        input_grad,
        in_weight_grad,
        out_weight_grad,
        kernel_grad,
        sums[0],
        sums[1],
        sums[3:].reshape(hidden),
        sums[2],
    )


def solution(mesh):
    return jax.shard_map(
        per_device_fused if fits(mesh.shape["row"]) else per_device,
        mesh=mesh,
        in_specs=(
            P(("grp", "row"), None, None),
            P(("grp", "row"), None, None),
            P(),
            P(),
            P(),
            P("row", None),
            P(),
            P("row", None),
            P(),
        ),
        out_specs=(
            P(("grp", "row"), None, None),
            P(("grp", "row"), None, None),
            P(("grp", "row"), None),
            P(("grp", "row"), None),
            P("grp", None, None),
            P("grp"),
            P("grp"),
            P("grp"),
            P("grp"),
        ),
        check_vma=False,
    )
```

```python
import functools
import math

import jax
import jax.numpy as jnp
from jax import lax
from jax.experimental import pallas as pl
from jax.experimental.pallas import tpu as pltpu
from jax.sharding import PartitionSpec as P


def extended(block, sides, width):
    for axis, dim in sides:
        count = lax.axis_size(axis)
        forward = [(i, i + 1) for i in range(count - 1)]
        backward = [(target, source) for source, target in forward]
        low = lax.ppermute(
            lax.slice_in_dim(block, block.shape[dim] - width, None, axis=dim), axis, forward
        )
        high = lax.ppermute(lax.slice_in_dim(block, 0, width, axis=dim), axis, backward)
        block = jnp.concatenate([low, block, high], axis=dim)
    return block


def conv_taps(padded, kernel, row_count, col_count):
    running = jnp.zeros((row_count, col_count, padded.shape[2]), jnp.float32)
    for tap_row in range(7):
        for tap_col in range(7):
            running = (
                running
                + padded[tap_row : tap_row + row_count, tap_col : tap_col + col_count]
                * kernel[tap_row, tap_col]
            )
    return running


def contract_last(left, right):
    return lax.dot_general(
        left, right, (((1,), (1,)), ((), ())), preferred_element_type=jnp.float32
    )


def contract_first(left, right):
    return lax.dot_general(
        left, right, (((0,), (0,)), ((), ())), preferred_element_type=jnp.float32
    )


def per_device(
    features, cotangent, kernel, norm_gain, norm_bias, in_weight, in_bias, out_weight, layer_scale
):
    row_count, col_count, channels = features.shape
    hidden_count = in_weight.shape[1]
    norm_scale = 1.0 / math.sqrt(row_count * col_count * lax.axis_size("row"))
    rimmed = extended(features, (("row", 0),), 3)
    padded = jnp.pad(rimmed, ((0, 0), (3, 3), (0, 0)))
    convolved = conv_taps(padded, kernel, row_count, col_count).reshape(-1, channels)
    average = jnp.mean(convolved, axis=1, keepdims=True)
    centred = convolved - average
    inv_std = lax.rsqrt(jnp.mean(centred * centred, axis=1, keepdims=True) + 1e-06)
    normed = centred * inv_std
    normed_out = (normed * norm_gain + norm_bias).astype(jnp.bfloat16)
    in_narrow = in_weight.astype(jnp.bfloat16)
    out_narrow = out_weight.astype(jnp.bfloat16)

    def fold_rows(left, piece):
        return jnp.dot(left, piece, preferred_element_type=jnp.float32)

    def map_rows(left, piece):
        return contract_last(left, piece)

    preact = fold_rows(normed_out, lax.all_gather(in_narrow, "row", axis=0, tiled=True)) + in_bias
    cdf_value = 0.5 * (1.0 + jax.scipy.special.erf(preact * 0.7071067811865476))
    activated = (preact * cdf_value).astype(jnp.bfloat16)
    mixed = map_rows(activated, lax.all_gather(out_narrow, "row", axis=0, tiled=True))
    flat_input = features.reshape(-1, channels)
    flat_cotan = cotangent.reshape(-1, channels)
    output = (flat_input + layer_scale * mixed).reshape(row_count, col_count, channels)
    scale_term = jnp.sum(flat_cotan * mixed, axis=0)
    branch_grad = (layer_scale * flat_cotan).astype(jnp.bfloat16)
    act_grad = fold_rows(branch_grad, lax.all_gather(out_narrow, "row", axis=0, tiled=True))
    gelu_slope = cdf_value + preact * jnp.exp(-0.5 * preact * preact) * 0.3989422804014327
    hidden_grad = act_grad * gelu_slope
    in_bias_term = jnp.sum(hidden_grad, axis=0)
    hidden_narrow = hidden_grad.astype(jnp.bfloat16)
    out_grad = map_rows(hidden_narrow, lax.all_gather(in_narrow, "row", axis=0, tiled=True))
    gain_term = jnp.sum(out_grad * normed, axis=0)
    bias_term = jnp.sum(out_grad, axis=0)
    normed_grad = out_grad * norm_gain
    conv_grad = inv_std * (
        normed_grad
        - jnp.mean(normed_grad, axis=1, keepdims=True)
        - normed * jnp.mean(normed_grad * normed, axis=1, keepdims=True)
    )
    grad_pairs = lax.psum_scatter(
        jnp.concatenate(
            [
                norm_scale * contract_first(normed_out, hidden_narrow),
                norm_scale * contract_first(branch_grad, activated),
            ],
            axis=1,
        ),
        "row",
        scatter_dimension=0,
        tiled=True,
    )
    in_weight_grad = grad_pairs[:, :hidden_count]
    out_weight_grad = grad_pairs[:, hidden_count:]
    conv_grid = conv_grad.reshape(row_count, col_count, channels)
    grad_rimmed = extended(conv_grid, (("row", 0),), 3)
    grad_padded = jnp.pad(grad_rimmed, ((0, 0), (3, 3), (0, 0)))
    input_grad = cotangent
    kernel_rows = []
    for tap_row in range(7):
        tap_list = []
        for tap_col in range(7):
            input_grad = (
                input_grad
                + kernel[tap_row, tap_col]
                * grad_padded[
                    6 - tap_row : 6 - tap_row + row_count, 6 - tap_col : 6 - tap_col + col_count
                ]
            )
            tap_list.append(
                jnp.sum(
                    padded[tap_row : tap_row + row_count, tap_col : tap_col + col_count]
                    * conv_grid,
                    axis=(0, 1),
                )
            )
        kernel_rows.append(jnp.stack(tap_list))
    kernel_term = norm_scale * jnp.stack(kernel_rows)
    small_sums = lax.psum(
        (
            kernel_term,
            norm_scale * gain_term,
            norm_scale * bias_term,
            norm_scale * in_bias_term,
            norm_scale * scale_term,
        ),
        "row",
    )
    return (
        output,
        input_grad,
        in_weight_grad,
        out_weight_grad,
        small_sums[0],
        small_sums[1],
        small_sums[2],
        small_sums[3],
        small_sums[4],
    )


F32, BF16 = jnp.float32, jnp.bfloat16
MESH = pl.DeviceIdType.MESH
CORES, XS = 2, 2
LANES = 128
EDGE = 8


def fits(count):
    planes = count // (CORES * XS)
    return count % (CORES * XS) == 0 and planes == 4


def per_device_fused(
    features, cotangent, kernel, norm_gain, norm_bias, in_weight, in_bias, out_weight, layer_scale
):
    count = lax.axis_size("row")
    planes = count // (CORES * XS)
    rows, cols, channels = features.shape
    own, hidden = in_weight.shape
    pixels = rows * cols
    taps = kernel.shape[0]
    rim = taps // 2
    wide = cols + 2 * EDGE
    chunk = channels
    pieces = hidden // chunk
    tap_total = taps * taps
    bias_rows = hidden // channels
    small_rows = tap_total + 3 + bias_rows
    norm_scale = 1.0 / math.sqrt(pixels * count)

    def body(
        feat, cot, kern, gain, beta, w_in, b_in, w_out, scale,
        out, in_grad, gw_in, gw_out, taps_out, small_out,
        weights, grads, from_core, x_send, from_x, z_send, from_up, from_down,
        padded, grad_padded, grad_edge, feat_edge, edge_in, conv, normed_s, inv_s, no_s, no_t, bg_s, bg_t, mixed_s, og_s,
        small, from_small,
        s_ag, r_ag, s_core, r_core, s_x, r_x, s_z, r_up, r_down,
        s_halo, r_halo, s_ghalo, r_ghalo, s_small, r_small,
    ):
        me = lax.axis_index("row")
        core = lax.rem(me, CORES)
        xpos = lax.rem(me // CORES, XS)
        z = me // (CORES * XS)
        sibling = me + 1 - 2 * core
        across = me + CORES - 2 * CORES * xpos
        step_z = CORES * XS

        def at(zz, xx, cc):
            return (zz * XS + xx) * CORES + cc

        def copy(src, dst, send, recv, target):
            return pltpu.make_async_remote_copy(
                src_ref=src, dst_ref=dst, send_sem=send, recv_sem=recv,
                device_id={"row": target}, device_id_type=MESH,
            )

        has_up, has_down = z < planes - 1, z > 0
        has_next, has_prev = me < count - 1, me > 0
        far_z = z + 2 - 4 * lax.rem(z // 2, 2)
        near_z = z + 1 - 2 * lax.rem(z, 2)
        far, near = at(far_z, xpos, core), at(near_z, xpos, core)

        feat_edge[...] = feat[...].astype(BF16)
        weights[0, me] = w_in[...].astype(BF16)
        weights[1, me] = w_out[...].astype(BF16)

        barrier = pltpu.get_barrier_semaphore()

        def greet(target):
            pl.semaphore_signal(barrier, inc=1, device_id={"row": target}, device_id_type=MESH)

        outer = lax.rem(me + count + 2 * core - 1, count)
        peers = [sibling, across, outer]
        peers += [at(lax.rem(z + d, planes), xpos, core) for d in range(1, planes)]
        for target in peers:
            greet(target)
        pl.semaphore_wait(barrier, len(peers))

        halo_next = copy(
            feat_edge.at[rows - rim :], edge_in.at[0],
            s_halo.at[0], r_halo.at[0], lax.rem(me + 1, count),
        )
        halo_prev = copy(
            feat_edge.at[0:rim], edge_in.at[1],
            s_halo.at[1], r_halo.at[1], lax.rem(me + count - 1, count),
        )

        @pl.when(has_next)
        def _():
            halo_next.start()

        @pl.when(has_prev)
        def _():
            halo_prev.start()

        def block(r):
            return weights.at[:, r]

        def ag(r, way, target):
            return copy(block(r), block(r), s_ag.at[way, r], r_ag.at[r], target)

        def arrived(r):
            ag(r, 0, sibling).wait_recv()

        started = []

        def send_if(here, r, way, target):
            if here is True:
                ag(r, way, target).start()
            else:
                @pl.when(here)
                def _():
                    ag(r, way, target).start()
            started.append((here, r, way, target))

        send_if(has_up, me, 0, me + step_z)
        send_if(has_down, me, 1, me - step_z)
        send_if(True, me, 2, across)
        send_if(True, me, 3, sibling)

        def gather_line(d):
            for sign in (1, -1):
                zz = z - sign * d
                here = (zz >= 0) & (zz < planes)
                r = at(zz, xpos, core)
                onward = has_up if sign > 0 else has_down

                @pl.when(here)
                def _():
                    arrived(r)

                send_if(here & onward, r, 0 if sign > 0 else 1, me + sign * step_z)
                send_if(here, r, 2, across)
                send_if(here, r, 3, sibling)

        def gather_across(d):
            for sign in (1, -1) if d else (1,):
                zz = z - sign * d
                here = (zz >= 0) & (zz < planes)
                r = at(zz, 1 - xpos, core)

                @pl.when(here)
                def _():
                    arrived(r)

                send_if(here, r, 3, sibling)

        blank = jnp.zeros((rows + 2 * rim, EDGE, channels), F32)
        for pad in (padded, grad_padded):
            pad[:, 0:EDGE, :] = blank
            pad[:, EDGE + cols :, :] = blank
        no_rows = jnp.zeros((rim, cols, channels), F32)
        padded[rim : rim + rows, EDGE : EDGE + cols, :] = feat[...]
        for here, first in ((has_prev, 0), (has_next, rows + rim)):
            @pl.when(jnp.logical_not(here))
            def _():
                padded[first : first + rim, EDGE : EDGE + cols, :] = no_rows
                grad_padded[first : first + rim, EDGE : EDGE + cols, :] = no_rows
        scaled = scale[...] * cot[...].reshape(pixels, channels)
        bg_s[...] = scaled.astype(BF16)
        bg_t[...] = scaled.T.astype(BF16)

        @pl.when(has_prev)
        def _():
            halo_next.wait_recv()
            padded[0:rim, EDGE : EDGE + cols, :] = edge_in[0].astype(F32)

        @pl.when(has_next)
        def _():
            halo_prev.wait_recv()
            padded[rows + rim :, EDGE : EDGE + cols, :] = edge_in[1].astype(F32)

        def lanes_of(i):
            return pl.ds(pl.multiple_of(i * LANES, LANES), LANES)

        def tap_sums(source, lanes, flip, starts):
            sums = list(starts)
            for j in range(taps):
                shift = EDGE - rim + j
                lines = [source[q, shift : shift + cols, lanes] for q in range(rows + 2 * rim)]
                for i in range(taps):
                    ki, kj = (taps - 1 - i, taps - 1 - j) if flip else (i, j)
                    weight = kern[ki, kj : kj + 1, lanes]
                    for q in range(rows):
                        sums[q] = sums[q] + lines[q + i] * weight
            return sums

        def conv_step(i, carry):
            lanes = lanes_of(i)
            sums = tap_sums(padded, lanes, False, [jnp.zeros((cols, LANES), F32)] * rows)
            for q in range(rows):
                conv[q * cols : (q + 1) * cols, lanes] = sums[q]
            return carry

        lax.fori_loop(0, channels // LANES, conv_step, 0)
        gather_line(1)
        value = conv[...]
        centred = value - jnp.mean(value, axis=1, keepdims=True)
        inv_std = lax.rsqrt(jnp.mean(centred * centred, axis=1, keepdims=True) + 1e-06)
        normed = centred * inv_std
        normed_s[...] = normed
        inv_s[...] = jnp.broadcast_to(inv_std, inv_s.shape)
        rescaled = normed * gain[...] + beta[...]
        no_s[...] = rescaled.astype(BF16)
        no_t[...] = rescaled.T.astype(BF16)
        mixed_s[...] = jnp.zeros_like(mixed_s)
        og_s[...] = jnp.zeros_like(og_s)
        gather_across(0)
        for d in range(2, planes):
            gather_line(d)
            gather_across(d - 1)
        gather_across(planes - 1)
        for xx in (xpos, 1 - xpos):
            for zz in range(planes):
                arrived(at(zz, xx, 1 - core))

        def last_last(a, b):
            return lax.dot_general(a, b, (((1,), (1,)), ((), ())), preferred_element_type=F32)

        def mlp_step(p, carry):
            span = pl.ds(pl.multiple_of(p * chunk, chunk), chunk)
            win = weights[0, :, :, span].reshape(channels, chunk)
            wout = weights[1, :, :, span].reshape(channels, chunk)
            preact = jnp.dot(no_s[...], win, preferred_element_type=F32) + b_in[:, span]
            cdf = 0.5 * (1.0 + lax.erf(preact * 0.7071067811865476))
            activated = (preact * cdf).astype(BF16)
            act_grad = jnp.dot(bg_s[...], wout, preferred_element_type=F32)
            slope = cdf + preact * jnp.exp(-0.5 * preact * preact) * 0.3989422804014327
            hidden_grad = act_grad * slope
            small[pl.ds(tap_total + 3 + p, 1), :] = norm_scale * jnp.sum(
                hidden_grad, axis=0, keepdims=True
            )
            narrow = hidden_grad.astype(BF16)
            grads[:, 0, :, span] = (
                (norm_scale * jnp.dot(no_t[...], narrow, preferred_element_type=F32))
                .astype(BF16).reshape(count, own, chunk)
            )
            grads[:, 1, :, span] = (
                (norm_scale * jnp.dot(bg_t[...], activated, preferred_element_type=F32))
                .astype(BF16).reshape(count, own, chunk)
            )
            mixed_s[...] += last_last(activated, wout)
            og_s[...] += last_last(narrow, win)
            return carry

        lax.fori_loop(0, pieces, mlp_step, 0)

        order = []
        for d in range(planes - 1, 0, -1):
            for sign in (1, -1):
                zz = z + sign * d
                order.append((zz, (zz >= 0) & (zz < planes), sign))

        def each(run, xx):
            for zz, here, sign in order:
                @pl.when(here)
                def _():
                    run(zz, xx, sign)
            run(z, xx, 0)

        def core_copy(zz, xx):
            slot = zz * XS + xx
            return copy(
                grads.at[at(zz, xx, 1 - core)], from_core.at[slot],
                s_core.at[slot], r_core.at[slot], sibling,
            )

        def x_copy(zz):
            return copy(x_send.at[zz], from_x.at[zz], s_x.at[zz], r_x.at[zz], across)

        def up_copy(zz):
            return copy(
                z_send.at[zz], from_up.at[zz], s_z.at[zz], r_up.at[zz],
                at(lax.rem(z + 1, planes), xpos, core),
            )

        def down_copy(zz):
            return copy(
                z_send.at[zz], from_down.at[zz], s_z.at[zz], r_down.at[zz],
                at(lax.rem(z + planes - 1, planes), xpos, core),
            )

        far_order = order[: 2 * (planes - 2)]
        near_order = order[2 * (planes - 2) :]

        def each_of(entries, run, xx):
            for zz, here, sign in entries:
                @pl.when(here)
                def _():
                    run(zz, xx, sign)

        each(lambda zz, xx, sign: core_copy(zz, xx).start(), 1 - xpos)
        each(lambda zz, xx, sign: core_copy(zz, xx).start(), xpos)

        def pair_sum(zz, xx):
            core_copy(zz, xx).wait_recv()
            return grads[at(zz, xx, core)].astype(F32) + from_core[zz * XS + xx].astype(F32)

        def add_for_x(zz, xx, sign):
            x_send[zz] = pair_sum(zz, xx).astype(BF16)
            x_copy(zz).start()

        each_of(far_order, add_for_x, 1 - xpos)

        flat_cot = cot[...].reshape(pixels, channels)
        small[tap_total + 2 : tap_total + 3, :] = norm_scale * jnp.sum(
            flat_cot * mixed_s[...], axis=0, keepdims=True
        )
        out_grad = og_s[...]
        normed = normed_s[...]
        small[tap_total : tap_total + 1, :] = norm_scale * jnp.sum(
            out_grad * normed, axis=0, keepdims=True
        )
        small[tap_total + 1 : tap_total + 2, :] = norm_scale * jnp.sum(
            out_grad, axis=0, keepdims=True
        )
        normed_grad = out_grad * gain[...]
        conv_grad = inv_s[:, 0:1] * (
            normed_grad
            - jnp.mean(normed_grad, axis=1, keepdims=True)
            - normed * jnp.mean(normed_grad * normed, axis=1, keepdims=True)
        )
        grid = conv_grad.reshape(rows, cols, channels)
        grad_padded[rim : rim + rows, EDGE : EDGE + cols, :] = grid
        grad_edge[...] = grid.astype(BF16)
        ghalo_next = copy(
            grad_edge.at[rows - rim :], edge_in.at[2],
            s_ghalo.at[0], r_ghalo.at[0], lax.rem(me + 1, count),
        )
        ghalo_prev = copy(
            grad_edge.at[0:rim], edge_in.at[3],
            s_ghalo.at[1], r_ghalo.at[1], lax.rem(me + count - 1, count),
        )

        @pl.when(has_next)
        def _():
            ghalo_next.start()

        @pl.when(has_prev)
        def _():
            ghalo_prev.start()

        def kernel_step(i, carry):
            lanes = lanes_of(i)
            lines_grad = [
                grad_padded[rim + q, EDGE : EDGE + cols, lanes] for q in range(rows)
            ]
            for j in range(taps):
                shift = EDGE - rim + j
                lines = [padded[q, shift : shift + cols, lanes] for q in range(rows + 2 * rim)]
                for k in range(taps):
                    total = lines[k] * lines_grad[0]
                    for q in range(1, rows):
                        total = total + lines[k + q] * lines_grad[q]
                    t = k * taps + j
                    small[t : t + 1, lanes] = norm_scale * jnp.sum(total, axis=0, keepdims=True)
            return carry

        lax.fori_loop(0, channels // LANES, kernel_step, 0)

        hops = (sibling, across, near, far)

        def small_copy(h):
            return copy(
                small.at[h * small_pad : (h + 1) * small_pad], from_small.at[h],
                s_small.at[h], r_small.at[h], hops[h],
            )

        def small_add(h):
            small_copy(h).wait_recv()
            small[(h + 1) * small_pad : (h + 2) * small_pad] = (
                small[h * small_pad : (h + 1) * small_pad] + from_small[h]
            )
            if h + 1 < len(hops):
                small_copy(h + 1).start()

        small_copy(0).start()
        out[...] = feat[...] + (scale[...] * mixed_s[...]).reshape(rows, cols, channels)
        small_add(0)
        each_of(near_order, add_for_x, 1 - xpos)
        add_for_x(z, 1 - xpos, 0)

        def pass_on(zz, xx, sign):
            fed, arriving, leaving = (
                (has_down, up_copy(zz), up_copy(zz)) if sign > 0
                else (has_up, down_copy(zz), down_copy(zz))
            )
            slots = from_up if sign > 0 else from_down
            x_copy(zz).wait_recv()
            total = pair_sum(zz, xx) + from_x[zz].astype(F32)

            @pl.when(fed)
            def _():
                arriving.wait_recv()
                z_send[zz] = (total + slots[zz].astype(F32)).astype(BF16)

            @pl.when(jnp.logical_not(fed))
            def _():
                z_send[zz] = total.astype(BF16)

            leaving.start()

        each_of(far_order, pass_on, xpos)

        @pl.when(has_prev)
        def _():
            ghalo_next.wait_recv()
            grad_padded[0:rim, EDGE : EDGE + cols, :] = edge_in[2].astype(F32)

        @pl.when(has_next)
        def _():
            ghalo_prev.wait_recv()
            grad_padded[rows + rim :, EDGE : EDGE + cols, :] = edge_in[3].astype(F32)

        def back_step(i, carry):
            lanes = lanes_of(i)
            sums = tap_sums(grad_padded, lanes, True, [cot[q, :, lanes] for q in range(rows)])
            for q in range(rows):
                in_grad[q, :, lanes] = sums[q]
            return carry

        lax.fori_loop(0, channels // LANES, back_step, 0)
        small_add(1)
        small_add(2)
        each_of(near_order, pass_on, xpos)
        x_copy(z).wait_recv()
        mine = pair_sum(z, xpos) + from_x[z].astype(F32)
        gw_in[...] = mine[0]
        gw_out[...] = mine[1]

        def join(slots):
            gw_in[...] += slots[z, 0].astype(F32)
            gw_out[...] += slots[z, 1].astype(F32)

        small_add(3)
        last = 4 * small_pad
        for i in range(taps):
            taps_out[i] = small[last + i * taps : last + (i + 1) * taps]
        small_out[0 : small_rows - tap_total] = small[last + tap_total : last + small_rows]

        @pl.when(has_down)
        def _():
            up_copy(z).wait_recv()
            join(from_up)

        @pl.when(has_up)
        def _():
            down_copy(z).wait_recv()
            join(from_down)

        @pl.when(has_next)
        def _():
            halo_next.wait_send()
            ghalo_next.wait_send()

        @pl.when(has_prev)
        def _():
            halo_prev.wait_send()
            ghalo_prev.wait_send()

        for here, r, way, target in started:
            if here is True:
                ag(r, way, target).wait_send()
            else:
                @pl.when(here)
                def _():
                    ag(r, way, target).wait_send()
        for zz in range(planes):
            for xx in range(XS):
                core_copy(zz, xx).wait_send()
            x_copy(zz).wait_send()
        for zz, here, sign in order:
            @pl.when(here)
            def _():
                up_copy(zz).wait_send()
        for h in range(len(hops)):
            small_copy(h).wait_send()

    small_pad = -(-small_rows // 8) * 8
    vmem = pl.BlockSpec(memory_space=pltpu.VMEM)
    dma = pltpu.SemaphoreType.DMA
    whole = (rows + 2 * rim, wide, channels)
    pair = (2, own, hidden)
    results = pl.pallas_call(
        body,
        out_shape=(
            jax.ShapeDtypeStruct(features.shape, F32),
            jax.ShapeDtypeStruct(features.shape, F32),
            jax.ShapeDtypeStruct((own, hidden), F32),
            jax.ShapeDtypeStruct((own, hidden), F32),
            jax.ShapeDtypeStruct(kernel.shape, F32),
            jax.ShapeDtypeStruct((small_rows - tap_total, channels), F32),
        ),
        in_specs=[vmem] * 9,
        out_specs=[vmem] * 6,
        scratch_shapes=[
            pltpu.VMEM((2, count, own, hidden), BF16),
            pltpu.VMEM((count,) + pair, BF16),
            pltpu.VMEM((planes * XS,) + pair, BF16),
            pltpu.VMEM((planes,) + pair, BF16),
            pltpu.VMEM((planes,) + pair, BF16),
            pltpu.VMEM((planes,) + pair, BF16),
            pltpu.VMEM((planes,) + pair, BF16),
            pltpu.VMEM((planes,) + pair, BF16),
            pltpu.VMEM(whole, F32),
            pltpu.VMEM(whole, F32),
            pltpu.VMEM(features.shape, BF16),
            pltpu.VMEM(features.shape, BF16),
            pltpu.VMEM((4, rim, cols, channels), BF16),
            pltpu.VMEM((pixels, channels), F32),
            pltpu.VMEM((pixels, channels), F32),
            pltpu.VMEM((pixels, LANES), F32),
            pltpu.VMEM((pixels, channels), BF16),
            pltpu.VMEM((channels, pixels), BF16),
            pltpu.VMEM((pixels, channels), BF16),
            pltpu.VMEM((channels, pixels), BF16),
            pltpu.VMEM((pixels, channels), F32),
            pltpu.VMEM((pixels, channels), F32),
            pltpu.VMEM((5 * small_pad, channels), F32),
            pltpu.VMEM((4, small_pad, channels), F32),
            dma((4, count)),
            dma((count,)),
            dma((planes * XS,)),
            dma((planes * XS,)),
            dma((planes,)),
            dma((planes,)),
            dma((planes,)),
            dma((planes,)),
            dma((planes,)),
            dma((2,)),
            dma((2,)),
            dma((2,)),
            dma((2,)),
            dma((4,)),
            dma((4,)),
        ],
        compiler_params=pltpu.CompilerParams(collective_id=0, has_side_effects=True),
        name="convnext_block",
    )(
        features,
        cotangent,
        kernel,
        norm_gain.reshape(1, channels),
        norm_bias.reshape(1, channels),
        in_weight,
        in_bias.reshape(1, hidden),
        out_weight,
        layer_scale.reshape(1, channels),
    )
    output, input_grad, in_weight_grad, out_weight_grad, kernel_grad, sums = results
    return (
        output,
        input_grad,
        in_weight_grad,
        out_weight_grad,
        kernel_grad,
        sums[0],
        sums[1],
        sums[3:].reshape(hidden),
        sums[2],
    )


def solution(mesh):
    return jax.shard_map(
        per_device_fused if fits(mesh.shape["row"]) else per_device,
        mesh=mesh,
        in_specs=(
            P(("grp", "row"), None, None),
            P(("grp", "row"), None, None),
            P(),
            P(),
            P(),
            P("row", None),
            P(),
            P("row", None),
            P(),
        ),
        out_specs=(
            P(("grp", "row"), None, None),
            P(("grp", "row"), None, None),
            P(("grp", "row"), None),
            P(("grp", "row"), None),
            P("grp", None, None),
            P("grp"),
            P("grp"),
            P("grp"),
            P("grp"),
        ),
        check_vma=False,
    )
```
